256 devices in a mesh: sec: 4 (over y_lo, core), seq: 64 (over y_hi, z, x).
Axes of the slice: x: 4, y: 4 (y_hi: 2, y_lo: 2; y = y_hi * 2 + y_lo), z: 8, core: 2. Of those that a mesh axis runs over, the one named last changes fastest.
Arguments:
- embedded: bfloat16 [4, 8192, 2304], P('sec', 'seq'), may hold values from -6 to 6
- recent: bfloat16 [4, 3, 8192, 2304], P('sec', None, 'seq'), may hold values from -6 to 6
- query_depth: float32 [4, 2304], P('sec'), may hold values from -6 to 6
- depth_temp: float32 [4], P('sec'), may hold values from 24 to 80
- w_latent: bfloat16 [4, 2304, 512], P('sec'), may hold values from -0.125 to 0.125
- w_query: bfloat16 [4, 2304, 2048], P('sec', None, 'seq'), may hold values from -0.125 to 0.125
- w_uk: bfloat16 [4, 16, 128, 512], P('sec'), may hold values from -0.5 to 0.5
- attn_temp: float32 [4, 16], P('sec'), may hold values from 16 to 64
- w_uv: bfloat16 [4, 16, 512, 128], P('sec'), may hold values from -1 to 1
- w_out: bfloat16 [4, 2048, 2304], P('sec', 'seq'), may hold values from -0.25 to 0.25
- block_offsets: int32 [64], replicated, may hold values from 0 to 63, as said below
Outputs:
- block_out: bfloat16 [4, 8192, 2304], P('sec', 'seq')
The draws below stay inside these ranges and needn't reach their ends.
Inputs may be any that keep to these rules, and one draw needn't show every extreme that they name: `block_offsets`: entries g * 64 to g * 64 + 63 hold every number of 0 to 63 once, for each sequence g.
All inputs are finite; a program needn't handle non-finite values.
Results may differ from the reference program's by a relative error of at most 0.012.
Values may be sent and summed in bfloat16 or wider, within the bound.
A program may use at most 128 MiB of HBM per device.

```python
import math
import jax
import jax.numpy as jnp
from jax import lax

D = 2304
HEADS = 16
HDIM = 128
LAT = 512
ROWS = 128
SEQS = 1
SPAN = 64
SEQLEN = 8192
TOKENS = 8192
N_SEC = 4


def draw_block_offsets(key, part):
    group_keys = jax.random.split(jax.random.fold_in(key, 7), SEQS)
    orders = jax.vmap(lambda group_key: jax.random.permutation(group_key, SPAN))(group_keys)
    return orders.reshape(-1).astype(jnp.int32)


def levels(own_key, extent, cuts, smallest, top_value):
    level, own = 1.0, jax.random.fold_in(own_key, 6)
    for dim, shards_of in cuts:
        heights = jnp.exp(jax.random.uniform(jax.random.fold_in(own, dim), (shards_of,), jnp.float32, smallest / len(cuts), top_value / len(cuts)))
        level = level * jnp.repeat(heights, extent[dim] // shards_of).reshape([-1 if axis == dim else 1 for axis in range(len(extent))])
    return level


def scatter_about(rng, dims, deviation, most, shards=(), held_as=jnp.bfloat16):
    drawn = deviation * jax.random.normal(rng, dims, jnp.float32)
    if shards:
        drawn = drawn * levels(rng, dims, shards, -0.22, 0.18)
    return jnp.clip(drawn, -most, most).astype(held_as)


def setup_inputs(seed: int = 0) -> dict:
    streams_of = jax.random.split(jax.random.key(seed), 12)
    embedded = scatter_about(streams_of[0], (N_SEC, TOKENS, D), 1.0, 6.0, ((0, 4), (1, 64)))
    recent = scatter_about(streams_of[1], (N_SEC, N_SEC - 1, TOKENS, D), 1.0, 6.0, ((0, 4), (2, 64)))
    query_depth = scatter_about(streams_of[2], (N_SEC, D), 1.0, 6.0, ((0, 4),), jnp.float32)
    depth_temp = jnp.clip(jnp.exp(math.log(80.0) - 1.2039728 * jax.random.uniform(streams_of[3], (N_SEC,), jnp.float32) ** levels(streams_of[3], (N_SEC,), ((0, 4),), -0.2, 0.2)), 24.0, 80.0)
    w_latent = scatter_about(streams_of[4], (N_SEC, D, LAT), D ** -0.5, 0.125, ((0, 4),))
    w_query = scatter_about(streams_of[5], (N_SEC, D, HEADS * HDIM), D ** -0.5, 0.125, ((0, 4), (2, 64)))
    w_uk = scatter_about(streams_of[6], (N_SEC, HEADS, HDIM, LAT), HDIM ** -0.5, 0.5, ((0, 4),))
    attn_temp = jnp.clip(jnp.exp(math.log(64.0) - 1.3862944 * jax.random.uniform(streams_of[7], (N_SEC, HEADS), jnp.float32) ** levels(streams_of[7], (N_SEC, HEADS), ((0, 4),), -0.2, 0.2)), 16.0, 64.0)
    w_uv = scatter_about(streams_of[8], (N_SEC, HEADS, LAT, HDIM), (LAT // 16) ** -0.5, 1.0, ((0, 4),))
    w_out = scatter_about(streams_of[9], (N_SEC, HEADS * HDIM, D), (HEADS * HDIM // 4) ** -0.5, 0.25, ((0, 4), (1, 64)))
    block_offsets = draw_block_offsets(jax.random.fold_in(streams_of[11], 71), 0)
    return dict(embedded=embedded, recent=recent, query_depth=query_depth, depth_temp=depth_temp, w_latent=w_latent, w_query=w_query, w_uk=w_uk, attn_temp=attn_temp, w_uv=w_uv, w_out=w_out, block_offsets=block_offsets)


tiny_stabilizer = 1e-06

def rms_scale(values):
    return lax.rsqrt(lax.optimization_barrier(jnp.mean(values * values, axis=-1, keepdims=True)) + tiny_stabilizer)

def reference(embedded, recent, query_depth, depth_temp, w_latent, w_query, w_uk, attn_temp, w_uv, w_out, block_offsets):
    device_rows = jnp.arange(TOKENS, dtype=jnp.int32)
    owner_ids = device_rows // ROWS
    positions = block_offsets[owner_ids].astype(jnp.int32) * ROWS + device_rows % ROWS
    outputs = []
    for section in range(N_SEC):
        sources = [embedded[section]] + [recent[j - 1, section - j] for j in range(1, section + 1)]
        earlier_block_outputs = jnp.stack(sources).astype(jnp.float32)
        learned_probe_direction = query_depth[section].astype(jnp.float32)
        query_norm = lax.rsqrt(jnp.mean(learned_probe_direction * learned_probe_direction) + tiny_stabilizer) / D
        logits = depth_temp[section] * query_norm * lax.optimization_barrier(jnp.sum(earlier_block_outputs * learned_probe_direction, axis=-1)) * rms_scale(earlier_block_outputs)[..., 0]
        weights = jnp.exp(logits)
        mixed = lax.optimization_barrier(jnp.sum(weights[..., None] * earlier_block_outputs, axis=0)) / lax.optimization_barrier(jnp.sum(weights, axis=0))[:, None]
        inputs = mixed.astype(jnp.bfloat16)
        latent = jnp.dot(inputs, w_latent[section], preferred_element_type=jnp.float32)
        key_rows = (latent * rms_scale(latent)).astype(jnp.bfloat16)
        queries = jnp.dot(inputs, w_query[section], preferred_element_type=jnp.float32).astype(jnp.bfloat16)
        queries = queries.reshape(TOKENS, HEADS, HDIM)
        absorbed = jnp.einsum('thd,hdl->thl', queries.astype(jnp.float32), w_uk[section].astype(jnp.float32))
        scaled = (absorbed * rms_scale(absorbed) * attn_temp[section][None, :, None] / LAT).astype(jnp.bfloat16)
        contexts = []
        for group in range(SEQS):
            first_row = group * SEQLEN
            seq_keys = key_rows[first_row:first_row + SEQLEN]
            seq_pos = positions[first_row:first_row + SEQLEN]
            causal_mask = seq_pos[None, :] <= seq_pos[:, None]
            seq_queries = jnp.transpose(scaled[first_row:first_row + SEQLEN], (1, 0, 2))

            def single_head(head_query):
                scores = jnp.dot(head_query, seq_keys.T, preferred_element_type=jnp.float32)
                weighted = jnp.where(causal_mask, jnp.exp(scores), jnp.zeros_like(scores))
                denominator = lax.optimization_barrier(jnp.sum(weighted, axis=-1))
                numerator = jnp.dot(weighted.astype(jnp.bfloat16), seq_keys, preferred_element_type=jnp.float32)
                return (numerator / denominator[:, None]).astype(jnp.bfloat16)
            contexts.append(jnp.transpose(lax.map(single_head, seq_queries), (1, 0, 2)))
        context = jnp.concatenate(contexts, axis=0)
        head_out = jnp.einsum('thl,hld->thd', context.astype(jnp.float32), w_uv[section].astype(jnp.float32))
        head_out = head_out.astype(jnp.bfloat16).reshape(TOKENS, HEADS * HDIM)
        outputs.append(jnp.dot(head_out, w_out[section], preferred_element_type=jnp.float32).astype(jnp.bfloat16))
    return jnp.stack(outputs)
```

```python
import functools

import jax
import jax.numpy as jnp
from jax import lax
from jax.experimental import pallas as pl
from jax.experimental.pallas import tpu as pltpu
from jax.sharding import PartitionSpec as P

MESH = pl.DeviceIdType.MESH
EPS = 1e-06
NY, NZ, NX = 2, 8, 4
GROUP = NY * NZ


def place():
    sec = lax.axis_index("sec")
    seq = lax.axis_index("seq")
    return sec, seq // (NZ * NX), (seq // NX) % NZ, seq % NX


def seq_of(y, z, x):
    return (y * NZ + z) * NX + x


class Net:
    def __init__(self, ssem, rsem):
        self.ssem, self.rsem, self.count, self.sent = ssem, rsem, 0, []

    def number(self):
        self.count += 1
        return self.count - 1

    def copy(self, n, src, dst, dev):
        return pltpu.make_async_remote_copy(
            src_ref=src,
            dst_ref=dst,
            send_sem=self.ssem.at[n],
            recv_sem=self.rsem.at[n],
            device_id=dev,
            device_id_type=MESH,
        )

    def send(self, n, src, dst, dev):
        c = self.copy(n, src, dst, dev)
        c.start()
        self.sent.append(c)

    def got(self, n, dst, dev):
        self.copy(n, dst, dst, dev).wait_recv()

    def drain(self):
        for c in self.sent:
            c.wait_send()


def meet(devs):
    barrier = pltpu.get_barrier_semaphore()
    for d in devs:
        pl.semaphore_signal(barrier, inc=1, device_id=d, device_id_type=MESH)
    pl.semaphore_wait(barrier, len(devs))


def peers():
    sec, y, z, x = place()
    return dict(
        right=(sec, seq_of(y, z, (x + 1) % NX)),
        left=(sec, seq_of(y, z, (x + 3) % NX)),
        over=(sec, seq_of(y, z, (x + 2) % NX)),
        up=(sec, seq_of(y, (z + 1) % NZ, x)),
        down=(sec, seq_of(y, (z + 7) % NZ, x)),
        far=(sec, seq_of(1 - y, z, x)),
    )


def first_kernel(recent, wq, wo, relayed, wq_all, wo_all, ssem, rsem):
    sec, y, z, x = place()
    seq = seq_of(y, z, x)
    n_sec = lax.axis_size("sec")
    at = peers()
    group, rank = seq // GROUP, seq % GROUP
    owner = rank * NX + group
    source = x * GROUP + seq // NX
    mine = seq // NX
    barrier = pltpu.get_barrier_semaphore()
    for name in ("up", "down", "far"):
        pl.semaphore_signal(barrier, inc=1, device_id=at[name], device_id_type=MESH)
    for a in range(1, n_sec):
        pl.semaphore_signal(
            barrier, inc=1, device_id=(lax.rem(sec + a, n_sec), seq), device_id_type=MESH
        )
    away = owner != seq

    @pl.when(away)
    def _():
        pl.semaphore_signal(barrier, inc=1, device_id=(sec, source), device_id_type=MESH)

    pl.semaphore_wait(barrier, 3 + n_sec - 1 + away.astype(jnp.int32))

    net = Net(ssem, rsem)
    shifts = []
    for a in range(1, n_sec):
        n = net.number()
        ok = sec + a < n_sec
        c = net.copy(
            n, recent.at[a - 1], relayed.at[a - 1], (lax.rem(sec + a, n_sec), seq)
        )
        pl.when(ok)(c.start)
        shifts.append((a, ok, c, n))
    arrays = ((wq, wq_all), (wo, wo_all))
    moves = []
    for src, out in arrays:
        n = net.number()
        c = net.copy(n, src, out.at[rank], (sec, owner))
        own = pltpu.make_async_copy(src, out.at[mine], ssem.at[n])
        pl.when(away)(c.start)
        pl.when(jnp.logical_not(away))(own.start)
        moves.append((out, n, c, own))
    right_n = {}
    left_n = {}
    far_n = {}
    for i, (out, n, c, own) in enumerate(moves):
        spot = out.at[mine]

        @pl.when(away)
        def _():
            net.copy(n, spot, spot, (sec, source)).wait_recv()

        pl.when(jnp.logical_not(away))(own.wait)
        far_n[i] = net.number()
        net.send(far_n[i], spot, spot, at["far"])
        right_n[i, 0, 1] = net.number()
        net.send(right_n[i, 0, 1], spot, spot, at["up"])
        left_n[i, 0, 1] = net.number()
        net.send(left_n[i, 0, 1], spot, spot, at["down"])
    for i, (out, n, c, own) in enumerate(moves):
        spot = out.at[(1 - y) * NZ + z]
        net.got(far_n[i], spot, at["far"])
        right_n[i, 1, 1] = net.number()
        net.send(right_n[i, 1, 1], spot, spot, at["up"])
        left_n[i, 1, 1] = net.number()
        net.send(left_n[i, 1, 1], spot, spot, at["down"])
    for i, (out, n, c, own) in enumerate(moves):
        for k in range(1, 5):
            for d in range(2):
                yy = y if d == 0 else 1 - y
                if (i, d, k) in right_n:
                    spot = out.at[yy * NZ + lax.rem(z + NZ - k, NZ)]
                    net.got(right_n[i, d, k], spot, at["down"])
                    if k < (4 if d == 0 else 3):
                        right_n[i, d, k + 1] = net.number()
                        net.send(right_n[i, d, k + 1], spot, spot, at["up"])
                if (i, d, k) in left_n:
                    spot = out.at[yy * NZ + lax.rem(z + k, NZ)]
                    net.got(left_n[i, d, k], spot, at["up"])
                    if k < (3 if d == 0 else 4):
                        left_n[i, d, k + 1] = net.number()
                        net.send(left_n[i, d, k + 1], spot, spot, at["down"])
    for a, ok, c, n in shifts:
        pl.when(ok)(c.wait_send)
        back = net.copy(
            n,
            relayed.at[a - 1],
            relayed.at[a - 1],
            (lax.rem(sec + n_sec - a, n_sec), seq),
        )
        pl.when(sec >= a)(back.wait_recv)
    for out, n, c, own in moves:
        pl.when(away)(c.wait_send)
    net.drain()


N_FIRST = 3 + 2 + 2 * (1 + 14)


def first(recent, wq, wo):
    any_ = pl.BlockSpec(memory_space=pl.ANY)
    return pl.pallas_call(
        first_kernel,
        out_shape=(
            jax.ShapeDtypeStruct(recent.shape, recent.dtype),
            jax.ShapeDtypeStruct((GROUP,) + wq.shape, wq.dtype),
            jax.ShapeDtypeStruct((GROUP,) + wo.shape, wo.dtype),
        ),
        in_specs=[any_] * 3,
        out_specs=(any_,) * 3,
        scratch_shapes=[
            pltpu.SemaphoreType.DMA((N_FIRST,)),
            pltpu.SemaphoreType.DMA((N_FIRST,)),
        ],
        compiler_params=pltpu.CompilerParams(collective_id=0, has_side_effects=True),
        name="shift_and_weights",
    )(recent, wq, wo)


def second_kernel(keys, mixed, keys_all, mixed_all, ssem, rsem, lsem):
    sec, y, z, x = place()
    at = peers()
    meet([at[n] for n in ("right", "left", "over", "up", "down", "far")])
    net = Net(ssem, rsem)
    rows = keys.shape[0]
    half = rows // 2
    lo, hi = pl.ds(0, half), pl.ds(half, half)

    def slot(yy, zz, xx):
        return (yy * NZ + zz) * NX + xx

    def xs(i):
        return lax.rem(x + i, NX)

    me = slot(y, z, x)
    k_own = pltpu.make_async_copy(keys, keys_all.at[me], lsem.at[0])
    m_own = pltpu.make_async_copy(mixed, mixed_all.at[x], lsem.at[1])
    k_own.start()
    m_own.start()

    ax = {}
    for name in ("right", "left", "over"):
        ax[name] = net.number()
        net.send(ax[name], keys.at[lo], keys_all.at[me, lo], at[name])
    b_far = net.number()
    net.send(b_far, keys.at[hi], keys_all.at[me, hi], at["far"])
    a_far = [net.number() for _ in range(NX)]
    net.send(a_far[0], keys.at[lo], keys_all.at[me, lo], at["far"])
    up_n, down_n = {}, {}

    def onward(kind, c, k, src, spot, ways=3):
        last_up = (4 if c % 2 == 0 else 3)
        last_down = 7 - last_up
        if ways & 1 and k <= last_up:
            up_n[kind, c, k] = net.number()
            net.send(up_n[kind, c, k], src, spot, at["up"])
        if ways & 2 and k <= last_down:
            down_n[kind, c, k] = net.number()
            net.send(down_n[kind, c, k], src, spot, at["down"])

    onward("b", 0, 1, keys.at[hi], keys_all.at[me, hi])
    onward("a", 0, 1, keys.at[lo], keys_all.at[me, lo])
    mx = {}
    for name in ("right", "left"):
        for h, part in ((0, lo), (1, hi)):
            mx[name, h] = net.number()
            net.send(mx[name, h], mixed.at[part], mixed_all.at[x, part], at[name])
    bx = {}

    def side(c, k, src, spot):
        for name in ("right", "left"):
            bx[c, k, name] = net.number()
            net.send(bx[c, k, name], src, spot, at[name])

    side(0, 0, keys.at[hi], keys_all.at[me, hi])
    a_x = {0: x, 1: xs(3), 2: xs(1), 3: xs(2)}
    for i, (name, back) in enumerate(
        (("right", "left"), ("left", "right"), ("over", "over")), start=1
    ):
        spot = keys_all.at[slot(y, z, a_x[i]), lo]
        net.got(ax[name], spot, at[back])
        net.send(a_far[i], spot, spot, at["far"])
        onward("a", i, 1, spot, spot)
    spot = keys_all.at[slot(1 - y, z, x), hi]
    net.got(b_far, spot, at["far"])
    onward("b", 1, 1, spot, spot)
    side(1, 0, spot, spot)
    for i in range(NX):
        spot = keys_all.at[slot(1 - y, z, a_x[i]), lo]
        net.got(a_far[i], spot, at["far"])
        onward("a", NX + i, 1, spot, spot)
    spot = mixed_all.at[xs(3), lo]
    net.got(mx["right", 0], spot, at["left"])
    m_up = net.number()
    net.send(m_up, spot, spot, at["right"])
    spot = mixed_all.at[xs(1), hi]
    net.got(mx["left", 1], spot, at["right"])
    m_down = net.number()
    net.send(m_down, spot, spot, at["left"])

    bxx = {}

    def relay(c, yy, zz, k):
        r = keys_all.at[slot(yy, zz, xs(3)), hi]
        l = keys_all.at[slot(yy, zz, xs(1)), hi]
        net.got(bx[c, k, "right"], r, at["left"])
        net.got(bx[c, k, "left"], l, at["right"])
        bxx[c, k] = net.number()
        if (c + k) % 2 == 0:
            net.send(bxx[c, k], r, r, at["right"])
        else:
            net.send(bxx[c, k], l, l, at["left"])

    def ended(c, yy, zz, k):
        net.got(
            bxx[c, k],
            keys_all.at[slot(yy, zz, xs(2)), hi],
            at["left"] if (c + k) % 2 == 0 else at["right"],
        )

    todo = [(0, y, z, 0), (1, 1 - y, z, 0)]
    tail = []
    for k in range(1, 5):
        fresh = []
        for kind, n_c, part in (("b", 2, hi), ("a", 2 * NX, lo)):
            for c in range(n_c):
                if kind == "b":
                    yy, xx = (y if c == 0 else 1 - y), x
                else:
                    yy, xx = (y if c < NX else 1 - y), a_x[c % NX]
                for table, back, zz, way in (
                    (up_n, "down", lax.rem(z + NZ - k, NZ), 1),
                    (down_n, "up", lax.rem(z + k, NZ), 2),
                ):
                    if (kind, c, k) not in table:
                        continue
                    spot = keys_all.at[slot(yy, zz, xx), part]
                    net.got(table[kind, c, k], spot, at[back])
                    onward(kind, c, k + 1, spot, spot, way)
                    if kind == "b":
                        tag = k if way == 1 else -k
                        side(c, tag, spot, spot)
                        fresh.append((c, yy, zz, tag))
            if kind == "b":
                for job in todo:
                    relay(*job)
                tail += todo
                todo = fresh
    for job in todo:
        relay(*job)
    tail += todo
    for job in tail:
        ended(*job)
    net.got(mx["right", 1], mixed_all.at[xs(3), hi], at["left"])
    net.got(mx["left", 0], mixed_all.at[xs(1), lo], at["right"])
    net.got(m_up, mixed_all.at[xs(2), lo], at["left"])
    net.got(m_down, mixed_all.at[xs(2), hi], at["right"])
    k_own.wait()
    m_own.wait()
    net.drain()
    assert net.count == N_SECOND, net.count


N_SECOND = 3 + 4 + 56 + 1 + 14 + 48 + 6


def second(keys, mixed):
    any_ = pl.BlockSpec(memory_space=pl.ANY)
    return pl.pallas_call(
        second_kernel,
        out_shape=(
            jax.ShapeDtypeStruct((NY * NZ * NX,) + keys.shape, keys.dtype),
            jax.ShapeDtypeStruct((NX,) + mixed.shape, mixed.dtype),
        ),
        in_specs=[any_] * 2,
        out_specs=(any_,) * 2,
        scratch_shapes=[
            pltpu.SemaphoreType.DMA((N_SECOND,)),
            pltpu.SemaphoreType.DMA((N_SECOND,)),
            pltpu.SemaphoreType.DMA((2,)),
        ],
        compiler_params=pltpu.CompilerParams(collective_id=1, has_side_effects=True),
        name="keys_and_rows",
    )(keys, mixed)


TILE = 4


def attend_kernel(
    pos, where, temps, mixed, wq, uk, keys, uv, wo, out,
    mixed_v, wq_v, uk_v, kv, uv_v, wo_v, scaled, acc, den, ho, sems, ksem,
):
    n_x, rows, width = mixed.shape
    heads, hdim, lat = uk.shape
    group_rows = heads * rows
    loads = [
        pltpu.make_async_copy(a, b, sems.at[i])
        for i, (a, b) in enumerate(
            ((mixed, mixed_v), (wq, wq_v), (uk, uk_v), (uv, uv_v), (wo, wo_v))
        )
    ]
    for i in range(3):
        loads[i].start()
    top = pos[0]
    for i in range(1, n_x):
        top = jnp.maximum(top, pos[i])
    tiles = top // TILE + 1

    def fetch(p, _):
        pltpu.make_async_copy(keys.at[where[p]], kv.at[p], ksem.at[p]).start()
        return 0

    lax.fori_loop(0, tiles * TILE, fetch, 0)
    loads[3].start()
    loads[4].start()
    for i in range(3):
        loads[i].wait()
    for b in range(n_x):
        q = lax.dot_general(
            mixed_v[b], wq_v[...], (((1,), (1,)), ((), ())),
            preferred_element_type=jnp.float32,
        ).astype(jnp.bfloat16)
        for h in range(heads):
            a = jnp.dot(
                q[:, h * hdim:(h + 1) * hdim], uk_v[h], preferred_element_type=jnp.float32
            )
            r = lax.rsqrt(jnp.mean(a * a, axis=-1, keepdims=True) + EPS)
            scaled[b, pl.ds(h * rows, rows), :] = (a * r * temps[h] / lat).astype(
                jnp.bfloat16
            )
    acc[...] = jnp.zeros_like(acc)
    den[...] = jnp.zeros_like(den)

    def step(t, _):
        for j in range(TILE):
            pltpu.make_async_copy(
                keys.at[0], kv.at[t * TILE + j], ksem.at[t * TILE + j]
            ).wait()
        n_k = TILE * rows

        def piece(b, r0, n_r, masked):
            k = kv[pl.ds(t * TILE, TILE)].reshape(n_k, lat)
            s = lax.dot_general(
                scaled[b, pl.ds(r0, n_r), :], k, (((1,), (1,)), ((), ())),
                preferred_element_type=jnp.float32,
            )
            p = jnp.exp(s)
            if masked:
                row = lax.broadcasted_iota(jnp.int32, (n_r, n_k), 0) % rows
                col = lax.broadcasted_iota(jnp.int32, (n_r, n_k), 1)
                p = jnp.where(col + t * n_k <= row + pos[b] * rows, p, 0.0)
            d = p[:, 0:128]
            for c in range(1, n_k // 128):
                d = d + p[:, c * 128:(c + 1) * 128]
            den[b, pl.ds(r0, n_r), :] += d
            acc[b, pl.ds(r0, n_r), :] += jnp.dot(
                p.astype(jnp.bfloat16), k, preferred_element_type=jnp.float32
            )

        for b in range(n_x):
            last = pos[b] // TILE

            @pl.when(t < last)
            def _():
                for r0 in range(0, group_rows, 256):
                    piece(b, r0, 256, False)

            @pl.when(t == last)
            def _():
                for r0 in range(0, group_rows, 256):
                    piece(b, r0, 256, True)

        return 0

    lax.fori_loop(0, tiles, step, 0)
    loads[3].wait()
    loads[4].wait()
    for b in range(n_x):
        for h in range(heads):
            part = pl.ds(h * rows, rows)
            d = jnp.sum(den[b, part, :], axis=-1, keepdims=True)
            ctx = (acc[b, part, :] / d).astype(jnp.bfloat16)
            ho[:, h * hdim:(h + 1) * hdim] = jnp.dot(
                ctx, uv_v[h], preferred_element_type=jnp.float32
            ).astype(jnp.bfloat16)
        out[b] = jnp.dot(
            ho[...], wo_v[...], preferred_element_type=jnp.float32
        ).astype(out.dtype)


def attend(pos, where, temps, mixed_all, wq, uk, keys_all, uv, wo):
    n_x, rows, width = mixed_all.shape
    heads, hdim, lat = uk.shape
    any_ = pl.BlockSpec(memory_space=pl.ANY)
    smem = pl.BlockSpec(memory_space=pltpu.SMEM)
    bf, f32 = jnp.bfloat16, jnp.float32
    return pl.pallas_call(
        attend_kernel,
        out_shape=jax.ShapeDtypeStruct((n_x, rows, width), bf),
        in_specs=[smem] * 3 + [any_] * 6,
        out_specs=pl.BlockSpec(memory_space=pltpu.VMEM),
        scratch_shapes=[
            pltpu.VMEM(mixed_all.shape, bf),
            pltpu.VMEM(wq.shape, bf),
            pltpu.VMEM(uk.shape, bf),
            pltpu.VMEM(keys_all.shape, bf),
            pltpu.VMEM(uv.shape, bf),
            pltpu.VMEM(wo.shape, bf),
            pltpu.VMEM((n_x, heads * rows, lat), bf),
            pltpu.VMEM((n_x, heads * rows, lat), f32),
            pltpu.VMEM((n_x, heads * rows, 128), f32),
            pltpu.VMEM((rows, heads * hdim), bf),
            pltpu.SemaphoreType.DMA((5,)),
            pltpu.SemaphoreType.DMA((keys_all.shape[0],)),
        ],
        compiler_params=pltpu.CompilerParams(vmem_limit_bytes=56 << 20),
        name="attend",
    )(pos, where, temps, mixed_all, wq, uk, keys_all, uv, wo)


def mix(embedded, relayed, sec, probe, temp):
    n = relayed.shape[0]
    ok = jnp.concatenate(
        [jnp.ones((1,), jnp.bool_), sec >= jnp.arange(1, n + 1, dtype=jnp.int32)]
    )
    stack = jnp.concatenate([embedded[None], relayed], axis=0)
    values = jnp.where(ok[:, None, None], stack, jnp.zeros_like(stack)).astype(jnp.float32)
    scale = lax.rsqrt(jnp.mean(probe * probe) + EPS) / probe.shape[0]
    norm = lax.rsqrt(jnp.mean(values * values, axis=-1) + EPS)
    logits = temp * scale * jnp.sum(values * probe, axis=-1) * norm
    weights = jnp.where(ok[:, None], jnp.exp(logits), 0.0)
    total = jnp.sum(weights, axis=0)
    return (jnp.sum(weights[..., None] * values, axis=0) / total[:, None]).astype(
        jnp.bfloat16
    )


def shards(
    embedded, recent, query_depth, depth_temp, w_latent, w_query, w_uk, attn_temp, w_uv,
    w_out, block_offsets,
):
    sec, y, z, x = place()
    n_dev = lax.axis_size("seq")
    rows = embedded.shape[1]
    relayed, wq_all, wo_all = first(recent[0], jnp.swapaxes(w_query[0], 0, 1), w_out[0])
    mixed = mix(embedded[0], relayed, sec, query_depth[0], depth_temp[0])
    latent = jnp.dot(mixed, w_latent[0], preferred_element_type=jnp.float32)
    keys = (
        latent * lax.rsqrt(jnp.mean(latent * latent, axis=-1, keepdims=True) + EPS)
    ).astype(jnp.bfloat16)
    keys_all, mixed_all = second(keys, mixed)
    ids = jnp.arange(n_dev, dtype=jnp.int32)
    where = jnp.sum(
        jnp.where(block_offsets[None, :] == ids[:, None], ids[None, :], 0), axis=1
    )
    base = (y * NZ + z) * NX
    pos = lax.dynamic_slice(block_offsets, (base,), (NX,))
    heads = w_uk.shape[1] // NX
    pick = functools.partial(lax.dynamic_slice_in_dim, start_index=x * heads, slice_size=heads)
    width = embedded.shape[2]
    partial = attend(
        pos, where, pick(attn_temp[0]), mixed_all, wq_all.reshape(-1, width),
        pick(w_uk[0]), keys_all, pick(w_uv[0]), wo_all.reshape(-1, width),
    )
    total = lax.dynamic_index_in_dim(partial, x, keepdims=False).astype(jnp.float32)
    for d in range(1, NX):
        pairs = [(i, i // NX * NX + (i + d) % NX) for i in range(n_dev)]
        block = lax.dynamic_index_in_dim(partial, (x + d) % NX, keepdims=False)
        total = total + lax.ppermute(block, "seq", pairs).astype(jnp.float32)
    return total.astype(jnp.bfloat16)[None]


def solution(mesh):
    in_specs = (
        P("sec", "seq", None),
        P("sec", None, "seq", None),
        P("sec", None),
        P("sec"),
        P("sec", None, None),
        P("sec", None, "seq"),
        P("sec", None, None, None),
        P("sec", None),
        P("sec", None, None, None),
        P("sec", "seq", None),
        P(),
    )
    return jax.shard_map(
        shards, mesh=mesh, in_specs=in_specs, out_specs=P("sec", "seq", None), check_vma=False
    )
```

```python
import functools

import jax
import jax.numpy as jnp
from jax import lax
from jax.experimental import pallas as pl
from jax.experimental.pallas import tpu as pltpu
from jax.sharding import PartitionSpec as P

MESH = pl.DeviceIdType.MESH
EPS = 1e-06
NY, NZ, NX = 2, 8, 4
GROUP = NY * NZ


def place():
    sec = lax.axis_index("sec")
    seq = lax.axis_index("seq")
    return sec, seq // (NZ * NX), (seq // NX) % NZ, seq % NX


def seq_of(y, z, x):
    return (y * NZ + z) * NX + x


class Net:
    def __init__(self, ssem, rsem):
        self.ssem, self.rsem, self.count, self.sent = ssem, rsem, 0, []

    def number(self):
        self.count += 1
        return self.count - 1

    def copy(self, n, src, dst, dev):
        return pltpu.make_async_remote_copy(
            src_ref=src,
            dst_ref=dst,
            send_sem=self.ssem.at[n],
            recv_sem=self.rsem.at[n],
            device_id=dev,
            device_id_type=MESH,
        )

    def send(self, n, src, dst, dev):
        c = self.copy(n, src, dst, dev)
        c.start()
        self.sent.append(c)

    def got(self, n, dst, dev):
        self.copy(n, dst, dst, dev).wait_recv()

    def drain(self):
        for c in self.sent:
            c.wait_send()


def meet(devs):
    barrier = pltpu.get_barrier_semaphore()
    for d in devs:
        pl.semaphore_signal(barrier, inc=1, device_id=d, device_id_type=MESH)
    pl.semaphore_wait(barrier, len(devs))


def peers():
    sec, y, z, x = place()
    return dict(
        right=(sec, seq_of(y, z, (x + 1) % NX)),
        left=(sec, seq_of(y, z, (x + 3) % NX)),
        over=(sec, seq_of(y, z, (x + 2) % NX)),
        up=(sec, seq_of(y, (z + 1) % NZ, x)),
        down=(sec, seq_of(y, (z + 7) % NZ, x)),
        far=(sec, seq_of(1 - y, z, x)),
    )


def first_kernel(recent, wq, wo, relayed, wq_all, wo_all, ssem, rsem):
    sec, y, z, x = place()
    seq = seq_of(y, z, x)
    n_sec = lax.axis_size("sec")
    at = peers()
    group, rank = seq // GROUP, seq % GROUP
    owner = rank * NX + group
    source = x * GROUP + seq // NX
    mine = seq // NX
    barrier = pltpu.get_barrier_semaphore()
    for name in ("up", "down", "far"):
        pl.semaphore_signal(barrier, inc=1, device_id=at[name], device_id_type=MESH)
    for a in range(1, n_sec):
        pl.semaphore_signal(
            barrier, inc=1, device_id=(lax.rem(sec + a, n_sec), seq), device_id_type=MESH
        )
    away = owner != seq

    @pl.when(away)
    def _():
        pl.semaphore_signal(barrier, inc=1, device_id=(sec, source), device_id_type=MESH)

    pl.semaphore_wait(barrier, 3 + n_sec - 1 + away.astype(jnp.int32))

    net = Net(ssem, rsem)
    shifts = []
    for a in range(1, n_sec):
        n = net.number()
        ok = sec + a < n_sec
        c = net.copy(
            n, recent.at[a - 1], relayed.at[a - 1], (lax.rem(sec + a, n_sec), seq)
        )
        pl.when(ok)(c.start)
        shifts.append((a, ok, c, n))
    arrays = ((wq, wq_all, 0), (wo, wo_all, y * NZ))
    moves = []
    for i, (src, out, base) in enumerate(arrays):
        n = net.number()
        there = rank if i == 0 else lax.rem(rank, NZ)
        c = net.copy(n, src, out.at[there], (sec, owner))
        own = pltpu.make_async_copy(src, out.at[mine - base], ssem.at[n])
        pl.when(away)(c.start)
        pl.when(jnp.logical_not(away))(own.start)
        moves.append((out, n, c, own, base))
    right_n = {}
    left_n = {}
    far_n = {}
    for i, (out, n, c, own, base) in enumerate(moves):
        spot = out.at[mine - base]

        @pl.when(away)
        def _():
            net.copy(n, spot, spot, (sec, source)).wait_recv()

        pl.when(jnp.logical_not(away))(own.wait)
        if i == 0:
            far_n[i] = net.number()
            net.send(far_n[i], spot, spot, at["far"])
        right_n[i, 0, 1] = net.number()
        net.send(right_n[i, 0, 1], spot, spot, at["up"])
        left_n[i, 0, 1] = net.number()
        net.send(left_n[i, 0, 1], spot, spot, at["down"])
    for i, (out, n, c, own, base) in enumerate(moves[:1]):
        spot = out.at[(1 - y) * NZ + z]
        net.got(far_n[i], spot, at["far"])
        right_n[i, 1, 1] = net.number()
        net.send(right_n[i, 1, 1], spot, spot, at["up"])
        left_n[i, 1, 1] = net.number()
        net.send(left_n[i, 1, 1], spot, spot, at["down"])
    for k in range(1, 5):
        for i, (out, n, c, own, base) in enumerate(moves):
            for d in range(2):
                yy = y if d == 0 else 1 - y
                if (i, d, k) in right_n:
                    spot = out.at[yy * NZ - base + lax.rem(z + NZ - k, NZ)]
                    net.got(right_n[i, d, k], spot, at["down"])
                    if k < (4 if d == 0 else 3):
                        right_n[i, d, k + 1] = net.number()
                        net.send(right_n[i, d, k + 1], spot, spot, at["up"])
                if (i, d, k) in left_n:
                    spot = out.at[yy * NZ - base + lax.rem(z + k, NZ)]
                    net.got(left_n[i, d, k], spot, at["up"])
                    if k < (3 if d == 0 else 4):
                        left_n[i, d, k + 1] = net.number()
                        net.send(left_n[i, d, k + 1], spot, spot, at["down"])
    for a, ok, c, n in shifts:
        pl.when(ok)(c.wait_send)
        back = net.copy(
            n,
            relayed.at[a - 1],
            relayed.at[a - 1],
            (lax.rem(sec + n_sec - a, n_sec), seq),
        )
        pl.when(sec >= a)(back.wait_recv)
    for out, n, c, own, base in moves:
        pl.when(away)(c.wait_send)
    net.drain()


N_FIRST = 3 + 2 + 1 + 14 + 7


def first(recent, wq, wo):
    any_ = pl.BlockSpec(memory_space=pl.ANY)
    return pl.pallas_call(
        first_kernel,
        out_shape=(
            jax.ShapeDtypeStruct(recent.shape, recent.dtype),
            jax.ShapeDtypeStruct((GROUP,) + wq.shape, wq.dtype),
            jax.ShapeDtypeStruct((NZ,) + wo.shape, wo.dtype),
        ),
        in_specs=[any_] * 3,
        out_specs=(any_,) * 3,
        scratch_shapes=[
            pltpu.SemaphoreType.DMA((N_FIRST,)),
            pltpu.SemaphoreType.DMA((N_FIRST,)),
        ],
        compiler_params=pltpu.CompilerParams(collective_id=0, has_side_effects=True),
        name="shift_and_weights",
    )(recent, wq, wo)


def main_kernel(
    bo, temps, keys, mixed, wq, uk, uv, wo_half, out,
    mixed_v, wq_v, uk_v, kv, uv_v, wo_v, scaled, acc, den, ho, po, passing, landed,
    ssem, rsem, lsem,
):
    sec, y, z, x = place()
    at = peers()
    rows, lat = keys.shape
    heads, hdim, _ = uk.shape
    width = mixed.shape[1]
    group_rows = heads * rows
    half = rows // 2
    lo, hi = pl.ds(0, half), pl.ds(half, half)
    f32, bf = jnp.float32, jnp.bfloat16

    def slot(yy, zz, xx):
        return (yy * NZ + zz) * NX + xx

    def xs(i):
        return lax.rem(x + i, NX)

    me = slot(y, z, x)
    wo_mine = pl.ds(y * NZ, NZ)
    loads = [
        pltpu.make_async_copy(a, b, lsem.at[i])
        for i, (a, b) in enumerate(
            (
                (wq, wq_v),
                (uk, uk_v),
                (keys, kv.at[me]),
                (uv, uv_v),
                (wo_half, wo_v.at[wo_mine]),
            )
        )
    ]
    for c in loads[:3]:
        c.start()
    meet([at[n] for n in ("right", "left", "over", "up", "down", "far")])
    net = Net(ssem, rsem)
    up_n, down_n, bx, bxx, ax, mx = {}, {}, {}, {}, {}, {}

    def onward(kind, c, k, src, spot, ways=3):
        last_up = 4 if c % 2 == 0 else 3
        last_down = 7 - last_up
        if ways & 1 and k <= last_up:
            up_n[kind, c, k] = net.number()
            net.send(up_n[kind, c, k], src, spot, at["up"])
        if ways & 2 and k <= last_down:
            down_n[kind, c, k] = net.number()
            net.send(down_n[kind, c, k], src, spot, at["down"])

    def side(c, k, src, spot):
        for name in ("right", "left"):
            bx[c, k, name] = net.number()
            net.send(bx[c, k, name], src, spot, at[name])

    def relay(c, yy, zz, k):
        r = kv.at[slot(yy, zz, xs(3)), hi]
        l = kv.at[slot(yy, zz, xs(1)), hi]
        net.got(bx[c, k, "right"], r, at["left"])
        net.got(bx[c, k, "left"], l, at["right"])
        bxx[c, k] = net.number()
        if (c + k) % 2 == 0:
            net.send(bxx[c, k], r, r, at["right"])
        else:
            net.send(bxx[c, k], l, l, at["left"])

    def ended(c, yy, zz, k):
        spot = kv.at[slot(yy, zz, xs(2)), hi]
        net.got(bxx[c, k], spot, at["left"] if (c + k) % 2 == 0 else at["right"])

    def tile_of(c, tag):
        yy = y if c == 0 else 1 - y
        return c, yy, lax.rem(z + NZ - tag, NZ), tag

    a_x = {0: x, 1: xs(3), 2: xs(1), 3: xs(2)}

    def piece(k, c, way):
        table, back = (up_n, "down") if way == 1 else (down_n, "up")
        tag = k if way == 1 else -k
        _, yy, zz, _ = tile_of(c, tag)
        if ("b", c, k) in table:
            spot = kv.at[slot(yy, zz, x), hi]
            net.got(table["b", c, k], spot, at[back])
            onward("b", c, k + 1, spot, spot, way)
            side(c, tag, spot, spot)
        for i in range(NX):
            n = ("a", c * NX + i, k)
            if n in table:
                spot = kv.at[slot(yy, zz, a_x[i]), lo]
                net.got(table[n], spot, at[back])
                onward("a", c * NX + i, k + 1, spot, spot, way)
        if k > 1:
            relay(*tile_of(c, (k - 1) * (1 if way == 1 else -1)))
        elif way == 1:
            relay(*tile_of(c, 0))

    for name in ("right", "left", "over"):
        ax[name] = net.number()
        net.send(ax[name], keys.at[lo], kv.at[me, lo], at[name])
    b_far = net.number()
    net.send(b_far, keys.at[hi], kv.at[me, hi], at["far"])
    a_far = [net.number() for _ in range(NX)]
    net.send(a_far[0], keys.at[lo], kv.at[me, lo], at["far"])
    onward("b", 0, 1, keys.at[hi], kv.at[me, hi])
    onward("a", 0, 1, keys.at[lo], kv.at[me, lo])
    for name in ("right", "left"):
        for h, part in ((0, lo), (1, hi)):
            if name == "left":
                h, part = 1 - h, (hi, lo)[h]
            mx[name, h] = net.number()
            net.send(mx[name, h], mixed.at[part], mixed_v.at[x, part], at[name])
    side(0, 0, keys.at[hi], kv.at[me, hi])
    for i, (name, back) in enumerate(
        (("right", "left"), ("left", "right"), ("over", "over")), start=1
    ):
        spot = kv.at[slot(y, z, a_x[i]), lo]
        net.got(ax[name], spot, at[back])
        net.send(a_far[i], spot, spot, at["far"])
        onward("a", i, 1, spot, spot)
    spot = kv.at[slot(1 - y, z, x), hi]
    net.got(b_far, spot, at["far"])
    onward("b", 1, 1, spot, spot)
    side(1, 0, spot, spot)
    for i in range(NX):
        spot = kv.at[slot(1 - y, z, a_x[i]), lo]
        net.got(a_far[i], spot, at["far"])
        onward("a", NX + i, 1, spot, spot)
    wo_far = net.number()
    net.send(wo_far, wo_half, wo_v.at[wo_mine], at["far"])
    for c in loads[3:]:
        c.start()

    for c in loads[:3]:
        c.wait()
    acc[...] = jnp.zeros_like(acc)
    den[...] = jnp.zeros_like(den)
    weights = wq_v[...].reshape(heads * hdim, width)

    def ask(b, source):
        q = lax.dot_general(
            source, weights, (((1,), (1,)), ((), ())), preferred_element_type=f32
        ).astype(bf)
        for h in range(heads):
            a = jnp.dot(q[:, h * hdim:(h + 1) * hdim], uk_v[h], preferred_element_type=f32)
            r = lax.rsqrt(jnp.mean(a * a, axis=-1, keepdims=True) + EPS)
            scaled[b, pl.ds(h * rows, rows), :] = (a * r * temps[h] / lat).astype(bf)

    gap = lax.broadcasted_iota(jnp.int32, (rows, rows), 1) - lax.broadcasted_iota(
        jnp.int32, (rows, rows), 0
    )

    def task(b, yy, zz):
        base = slot(yy, zz, 0)
        k = kv[pl.ds(base, NX)].reshape(NX * rows, lat)
        here = bo[slot(y, z, b)]
        limit = [(here - bo[base + j]) * rows for j in range(NX)]
        seen = [gap <= limit[j] for j in range(NX)]
        n_h = 2
        for h0 in range(0, heads, n_h):
            part = pl.ds(h0 * rows, n_h * rows)
            s = lax.dot_general(
                scaled[b, part, :], k, (((1,), (1,)), ((), ())), preferred_element_type=f32
            )
            p = jnp.exp(s)
            p = jnp.concatenate(
                [
                    jnp.concatenate(
                        [
                            jnp.where(
                                seen[j],
                                p[h * rows:(h + 1) * rows, j * rows:(j + 1) * rows],
                                0.0,
                            )
                            for j in range(NX)
                        ],
                        axis=1,
                    )
                    for h in range(n_h)
                ],
                axis=0,
            )
            d = p[:, 0:rows]
            for j in range(1, NX):
                d = d + p[:, j * rows:(j + 1) * rows]
            den[b, part, :] += d
            acc[b, part, :] += jnp.dot(p.astype(bf), k, preferred_element_type=f32)

    def first_tiles(b):
        def one(i, _):
            task(b, y + i * (1 - 2 * y), z)
            return 0

        lax.fori_loop(0, 2, one, 0)

    ask(x, mixed[...])
    piece(1, 0, 1)
    piece(1, 0, 2)
    piece(1, 1, 1)
    piece(1, 1, 2)
    spot = mixed_v.at[xs(3), lo]
    net.got(mx["right", 0], spot, at["left"])
    m_up = net.number()
    net.send(m_up, spot, spot, at["right"])
    spot = mixed_v.at[xs(1), hi]
    net.got(mx["left", 1], spot, at["right"])
    m_down = net.number()
    net.send(m_down, spot, spot, at["left"])
    ended(*tile_of(0, 0))
    ended(*tile_of(1, 0))
    first_tiles(x)
    net.got(mx["right", 1], mixed_v.at[xs(3), hi], at["left"])
    net.got(mx["left", 0], mixed_v.at[xs(1), lo], at["right"])
    for i in (3, 1):
        ask(xs(i), mixed_v[xs(i)])
        first_tiles(xs(i))
        piece(2, 0, 1 if i == 3 else 2)
    net.got(m_up, mixed_v.at[xs(2), lo], at["left"])
    net.got(m_down, mixed_v.at[xs(2), hi], at["right"])
    ask(xs(2), mixed_v[xs(2)])
    first_tiles(xs(2))

    turns = [(c, w) for c in range(2) for w in (1, 2)]
    plan = [(2, 1, 1), (2, 1, 2)]
    plan += [(3, c, w) for c, w in turns]
    plan += [(4, 0, 1), (4, 0, 2), (4, 1, 1), (4, 1, 2)]
    plan_at = 0
    for k in (1, 2):
        for j, (c, w) in enumerate(turns):
            take = 2 if k == 1 and j == 0 else 1
            for _ in range(take):
                if plan_at < len(plan):
                    piece(*plan[plan_at])
                    plan_at += 1
            tag = k if w == 1 else -k
            ended(*tile_of(c, tag))
            _, yy, zz, _ = tile_of(c, tag)

            def one(b, _, yy=yy, zz=zz):
                task(b, yy, zz)
                return 0

            lax.fori_loop(0, NX, one, 0)
    while plan_at < len(plan):
        piece(*plan[plan_at])
        plan_at += 1
    last = [(0, 4), (1, -4)]
    for c, tag in last:
        relay(*tile_of(c, tag))
    for c, w in turns:
        ended(*tile_of(c, 3 if w == 1 else -3))
    for c, tag in last:
        ended(*tile_of(c, tag))

    def last_tiles(b):
        def one(i, _):
            task(b, y + (i % 2) * (1 - 2 * y), lax.rem(z + 3 + i // 2, NZ))
            return 0

        lax.fori_loop(0, 6, one, 0)
        for h in range(heads):
            part = pl.ds(h * rows, rows)
            d = jnp.sum(den[b, part, :], axis=-1, keepdims=True)
            ctx = (acc[b, part, :] / d).astype(bf)
            ho[:, h * hdim:(h + 1) * hdim] = jnp.dot(
                ctx, uv_v[h], preferred_element_type=f32
            ).astype(bf)

    def project():
        return jnp.dot(
            ho[...], wo_v[...].reshape(heads * hdim, width), preferred_element_type=f32
        )

    loads[3].wait()
    last_tiles(xs(2))
    loads[4].wait()
    net.got(wo_far, wo_v.at[pl.ds((1 - y) * NZ, NZ)], at["far"])
    po[0] = project().astype(bf)
    out_n = [net.number() for _ in range(4)]
    net.send(out_n[0], po.at[0, lo], passing.at[0], at["right"])
    net.send(out_n[1], po.at[0, hi], passing.at[1], at["left"])
    last_tiles(xs(1))
    net.got(out_n[0], passing.at[0], at["left"])
    res = project()
    po[1, lo] = (res[:half] + passing[0].astype(f32)).astype(bf)
    po[1, hi] = res[half:].astype(bf)
    net.send(out_n[2], po.at[1], landed.at[0], at["right"])
    last_tiles(xs(3))
    net.got(out_n[1], passing.at[1], at["right"])
    res = project()
    po[2, lo] = res[:half].astype(bf)
    po[2, hi] = (res[half:] + passing[1].astype(f32)).astype(bf)
    net.send(out_n[3], po.at[2], landed.at[1], at["left"])
    last_tiles(x)
    res = project()
    net.got(out_n[2], landed.at[0], at["left"])
    net.got(out_n[3], landed.at[1], at["right"])
    out[...] = (res + landed[0].astype(f32) + landed[1].astype(f32)).astype(out.dtype)
    net.drain()
    assert net.count == N_MAIN, net.count


N_MAIN = 3 + 4 + 56 + 1 + 14 + 48 + 6 + 1 + 4


def main(bo, temps, keys, mixed, wq, uk, uv, wo_half):
    rows, width = mixed.shape
    heads, hdim, lat = uk.shape
    any_ = pl.BlockSpec(memory_space=pl.ANY)
    smem = pl.BlockSpec(memory_space=pltpu.SMEM)
    vmem = pl.BlockSpec(memory_space=pltpu.VMEM)
    bf, f32 = jnp.bfloat16, jnp.float32
    n_dev = bo.shape[0]
    return pl.pallas_call(
        main_kernel,
        out_shape=jax.ShapeDtypeStruct((rows, width), bf),
        in_specs=[smem, smem, vmem, vmem, any_, any_, any_, any_],
        out_specs=vmem,
        scratch_shapes=[
            pltpu.VMEM((NX, rows, width), bf),
            pltpu.VMEM(wq.shape, bf),
            pltpu.VMEM(uk.shape, bf),
            pltpu.VMEM((n_dev, rows, lat), bf),
            pltpu.VMEM(uv.shape, bf),
            pltpu.VMEM((GROUP,) + wo_half.shape[1:], bf),
            pltpu.VMEM((NX, heads * rows, lat), bf),
            pltpu.VMEM((NX, heads * rows, lat), f32),
            pltpu.VMEM((NX, heads * rows, rows), f32),
            pltpu.VMEM((rows, heads * hdim), bf),
            pltpu.VMEM((3, rows, width), bf),
            pltpu.VMEM((2, rows // 2, width), bf),
            pltpu.VMEM((2, rows, width), bf),
            pltpu.SemaphoreType.DMA((N_MAIN,)),
            pltpu.SemaphoreType.DMA((N_MAIN,)),
            pltpu.SemaphoreType.DMA((5,)),
        ],
        compiler_params=pltpu.CompilerParams(
            collective_id=1, has_side_effects=True, vmem_limit_bytes=60 << 20
        ),
        name="attend_and_sum",
    )(bo, temps, keys, mixed, wq, uk, uv, wo_half)


def mix(embedded, relayed, sec, probe, temp):
    n = relayed.shape[0]
    ok = jnp.concatenate(
        [jnp.ones((1,), jnp.bool_), sec >= jnp.arange(1, n + 1, dtype=jnp.int32)]
    )
    stack = jnp.concatenate([embedded[None], relayed], axis=0)
    values = jnp.where(ok[:, None, None], stack, jnp.zeros_like(stack)).astype(jnp.float32)
    scale = lax.rsqrt(jnp.mean(probe * probe) + EPS) / probe.shape[0]
    norm = lax.rsqrt(jnp.mean(values * values, axis=-1) + EPS)
    logits = temp * scale * jnp.sum(values * probe, axis=-1) * norm
    weights = jnp.where(ok[:, None], jnp.exp(logits), 0.0)
    total = jnp.sum(weights, axis=0)
    return (jnp.sum(weights[..., None] * values, axis=0) / total[:, None]).astype(
        jnp.bfloat16
    )


def shards(
    embedded, recent, query_depth, depth_temp, w_latent, w_query, w_uk, attn_temp, w_uv,
    w_out, block_offsets,
):
    sec, y, z, x = place()
    relayed, wq_all, wo_half = first(recent[0], jnp.swapaxes(w_query[0], 0, 1), w_out[0])
    mixed = mix(embedded[0], relayed, sec, query_depth[0], depth_temp[0])
    latent = jnp.dot(mixed, w_latent[0], preferred_element_type=jnp.float32)
    keys = (
        latent * lax.rsqrt(jnp.mean(latent * latent, axis=-1, keepdims=True) + EPS)
    ).astype(jnp.bfloat16)
    heads = w_uk.shape[1] // NX
    pick = functools.partial(lax.dynamic_slice_in_dim, start_index=x * heads, slice_size=heads)
    return main(
        block_offsets, pick(attn_temp[0]), keys, mixed, wq_all, pick(w_uk[0]),
        pick(w_uv[0]), wo_half,
    )[None]


def solution(mesh):
    in_specs = (
        P("sec", "seq", None),
        P("sec", None, "seq", None),
        P("sec", None),
        P("sec"),
        P("sec", None, None),
        P("sec", None, "seq"),
        P("sec", None, None, None),
        P("sec", None),
        P("sec", None, None, None),
        P("sec", "seq", None),
        P(),
    )
    return jax.shard_map(
        shards, mesh=mesh, in_specs=in_specs, out_specs=P("sec", "seq", None), check_vma=False
    )
```

```python
import functools

import jax
import jax.numpy as jnp
from jax import lax
from jax.experimental import pallas as pl
from jax.experimental.pallas import tpu as pltpu
from jax.sharding import PartitionSpec as P

MESH = pl.DeviceIdType.MESH
EPS = 1e-06
NY, NZ, NX = 2, 8, 4
GROUP = NY * NZ


def place():
    sec = lax.axis_index("sec")
    seq = lax.axis_index("seq")
    return sec, seq // (NZ * NX), (seq // NX) % NZ, seq % NX


def seq_of(y, z, x):
    return (y * NZ + z) * NX + x


class Net:
    def __init__(self, ssem, rsem):
        self.ssem, self.rsem, self.count, self.sent = ssem, rsem, 0, []

    def number(self):
        self.count += 1
        return self.count - 1

    def copy(self, n, src, dst, dev):
        return pltpu.make_async_remote_copy(
            src_ref=src,
            dst_ref=dst,
            send_sem=self.ssem.at[n],
            recv_sem=self.rsem.at[n],
            device_id=dev,
            device_id_type=MESH,
        )

    def send(self, n, src, dst, dev, like=None):
        self.copy(n, src, dst, dev).start()
        self.sent.append((n, src if like is None else like))

    def got(self, n, dst, dev):
        self.copy(n, dst, dst, dev).wait_recv()

    def drain(self, dev):
        for n, like in self.sent:
            self.copy(n, like, like, dev).wait_send()


def peers():
    sec, y, z, x = place()
    return dict(
        right=(sec, seq_of(y, z, (x + 1) % NX)),
        left=(sec, seq_of(y, z, (x + 3) % NX)),
        over=(sec, seq_of(y, z, (x + 2) % NX)),
        up=(sec, seq_of(y, (z + 1) % NZ, x)),
        down=(sec, seq_of(y, (z + 7) % NZ, x)),
        far=(sec, seq_of(1 - y, z, x)),
    )


def tick_kernel(
    bo, temps, depth_temp, embedded, probe, wq, wo, recent, w_latent, w_uk, w_uv, out,
    relayed, blend, weight, lat_v, wq_v, wo_v, uk_v, uv_v, mixed_v, kv,
    scaled, acc, den, ho, po, passing, landed, ssem, rsem, lsem,
):
    sec, y, z, x = place()
    seq = slot_me = seq_of(y, z, x)
    n_sec = lax.axis_size("sec")
    at = peers()
    rows, width = embedded.shape
    _, hdim, lat = w_uk.shape
    heads = w_uk.shape[0] // NX
    half = rows // 2
    lo, hi = pl.ds(0, half), pl.ds(half, half)
    f32, bf = jnp.float32, jnp.bfloat16

    def slot(yy, zz, xx):
        return (yy * NZ + zz) * NX + xx

    def xs(i):
        return lax.rem(x + i, NX)

    mine_heads = pl.ds(x * heads, heads)
    loads = [
        pltpu.make_async_copy(a, b, lsem.at[i])
        for i, (a, b) in enumerate(
            ((w_latent, lat_v), (w_uk.at[mine_heads], uk_v), (w_uv.at[mine_heads], uv_v))
        )
    ]
    for c in loads:
        c.start()

    group, rank = seq // GROUP, seq % GROUP
    owner = rank * NX + group
    source = x * GROUP + seq // NX
    mine = seq // NX
    away = owner != seq
    barrier = pltpu.get_barrier_semaphore()
    names = ("right", "left", "over", "up", "down", "far")
    for name in names:
        pl.semaphore_signal(barrier, inc=1, device_id=at[name], device_id_type=MESH)
    for a in range(1, n_sec):
        pl.semaphore_signal(
            barrier, inc=1, device_id=(lax.rem(sec + a, n_sec), seq), device_id_type=MESH
        )

    @pl.when(away)
    def _():
        pl.semaphore_signal(barrier, inc=1, device_id=(sec, source), device_id_type=MESH)

    pl.semaphore_wait(barrier, len(names) + n_sec - 1 + away.astype(jnp.int32))

    net = Net(ssem, rsem)

    moves = []
    for i, (src, dst, base, there) in enumerate(
        ((wq, wq_v, 0, rank), (wo, wo_v, 0, rank))
    ):
        n = net.number()
        c = net.copy(n, src, dst.at[there], (sec, owner))
        own = pltpu.make_async_copy(src, dst.at[mine], ssem.at[n])
        pl.when(away)(c.start)
        pl.when(jnp.logical_not(away))(own.start)
        moves.append((dst, n, c, own))
    shifts = []
    for a in range(1, n_sec):
        n = net.number()
        ok = sec + a < n_sec
        c = net.copy(
            n, recent.at[a - 1], relayed.at[a - 1], (lax.rem(sec + a, n_sec), seq)
        )
        pl.when(ok)(c.start)
        shifts.append((a, ok, c, n))
    ring_up, ring_down = {}, {}

    def ring(i, d, k, spot, ways=3):
        last_up = 4 if d == 0 else 3
        if ways & 1 and k <= last_up:
            ring_up[i, d, k] = net.number()
            net.send(ring_up[i, d, k], spot, spot, at["up"])
        if ways & 2 and k <= 7 - last_up:
            ring_down[i, d, k] = net.number()
            net.send(ring_down[i, d, k], spot, spot, at["down"])

    def ring_step(k):
        for i, (dst, n, c, own) in enumerate(moves):
            for d in range(2):
                yy = y if d == 0 else 1 - y
                if (i, d, k) in ring_up:
                    spot = dst.at[yy * NZ + lax.rem(z + NZ - k, NZ)]
                    net.got(ring_up[i, d, k], spot, at["down"])
                    ring(i, d, k + 1, spot, 1)
                if (i, d, k) in ring_down:
                    spot = dst.at[yy * NZ + lax.rem(z + k, NZ)]
                    net.got(ring_down[i, d, k], spot, at["up"])
                    ring(i, d, k + 1, spot, 2)

    q_far = net.number()
    for i, (dst, n, c, own) in enumerate(moves):
        spot = dst.at[mine]

        @pl.when(away)
        def _():
            net.copy(n, spot, spot, (sec, source)).wait_recv()

        pl.when(jnp.logical_not(away))(own.wait)
        if i == 0:
            net.send(q_far, spot, spot, at["far"])
        ring(i, 0, 1, spot)
    spot = wq_v.at[(1 - y) * NZ + z]
    net.got(q_far, spot, at["far"])
    ring(0, 1, 1, spot)
    ring_step(1)

    asked = probe[...]
    scale = (
        depth_temp[0] * lax.rsqrt(jnp.mean(asked * asked, axis=-1, keepdims=True) + EPS) / width
    )
    step_rows = 16

    def add_source(read, fresh):
        def some(i, _):
            part = pl.ds(pl.multiple_of(i * step_rows, step_rows), step_rows)
            v = read(part).astype(f32)
            norm = lax.rsqrt(jnp.mean(v * v, axis=-1, keepdims=True) + EPS)
            w = jnp.exp(scale * jnp.sum(v * asked, axis=-1, keepdims=True) * norm)
            if fresh:
                blend[part, :] = w * v
                weight[part, :] = jnp.broadcast_to(w, (step_rows, 128))
            else:
                blend[part, :] += w * v
                weight[part, :] += jnp.broadcast_to(w, (step_rows, 128))
            return 0

        lax.fori_loop(0, rows // step_rows, some, 0)

    add_source(lambda part: embedded[part, :], True)
    ring_step(2)
    for a, ok, c, n in shifts:

        @pl.when(sec >= a)
        def _():
            net.copy(
                n,
                relayed.at[a - 1],
                relayed.at[a - 1],
                (lax.rem(sec + n_sec - a, n_sec), seq),
            ).wait_recv()
            add_source(lambda part: relayed[a - 1, part, :], False)

    def finish(i, _):
        part = pl.ds(pl.multiple_of(i * step_rows, step_rows), step_rows)
        mixed_v[x, part, :] = (blend[part, :] / weight[part, 0:1]).astype(bf)
        return 0

    lax.fori_loop(0, rows // step_rows, finish, 0)
    loads[0].wait()
    latent = jnp.dot(mixed_v[x], lat_v[...], preferred_element_type=f32)
    kv[slot_me] = (
        latent * lax.rsqrt(jnp.mean(latent * latent, axis=-1, keepdims=True) + EPS)
    ).astype(bf)

    up_n, down_n, bx, bxx, ax, mx = {}, {}, {}, {}, {}, {}
    some_half = kv.at[0, lo]

    def onward(kind, c, k, spot, ways=3):
        last_up = 4 if c % 2 == 0 else 3
        if ways & 1 and k <= last_up:
            up_n[kind, c, k] = net.number()
            net.send(up_n[kind, c, k], spot, spot, at["up"], some_half)
        if ways & 2 and k <= 7 - last_up:
            down_n[kind, c, k] = net.number()
            net.send(down_n[kind, c, k], spot, spot, at["down"], some_half)

    def side(c, k, spot):
        for name in ("right", "left"):
            bx[c, k, name] = net.number()
            net.send(bx[c, k, name], spot, spot, at[name], some_half)

    def tile_of(c, tag):
        yy = y if c == 0 else 1 - y
        return c, yy, lax.rem(z + NZ - tag, NZ), tag

    def relay(c, tag):
        _, yy, zz, _ = tile_of(c, tag)
        r = kv.at[slot(yy, zz, xs(3)), hi]
        l = kv.at[slot(yy, zz, xs(1)), hi]
        net.got(bx[c, tag, "right"], r, at["left"])
        net.got(bx[c, tag, "left"], l, at["right"])
        bxx[c, tag] = net.number()
        if (c + tag) % 2 == 0:
            net.send(bxx[c, tag], r, r, at["right"], some_half)
        else:
            net.send(bxx[c, tag], l, l, at["left"], some_half)

    def ended(c, tag):
        _, yy, zz, _ = tile_of(c, tag)
        spot = kv.at[slot(yy, zz, xs(2)), hi]
        net.got(bxx[c, tag], spot, at["left"] if (c + tag) % 2 == 0 else at["right"])

    a_x = {0: x, 1: xs(3), 2: xs(1), 3: xs(2)}

    def piece(k, c, way):
        table, back = (up_n, "down") if way == 1 else (down_n, "up")
        tag = k if way == 1 else -k
        _, yy, zz, _ = tile_of(c, tag)
        if ("b", c, k) in table:
            spot = kv.at[slot(yy, zz, x), hi]
            net.got(table["b", c, k], spot, at[back])
            onward("b", c, k + 1, spot, way)
            side(c, tag, spot)
        for i in range(NX):
            n = ("a", c * NX + i, k)
            if n in table:
                spot = kv.at[slot(yy, zz, a_x[i]), lo]
                net.got(table[n], spot, at[back])
                onward("a", c * NX + i, k + 1, spot, way)

    ring_step(3)
    mine_lo, mine_hi = kv.at[slot_me, lo], kv.at[slot_me, hi]
    for name in ("right", "left", "over"):
        ax[name] = net.number()
        net.send(ax[name], mine_lo, mine_lo, at[name])
    b_far = net.number()
    net.send(b_far, mine_hi, mine_hi, at["far"])
    a_far = [net.number() for _ in range(NX)]
    net.send(a_far[0], mine_lo, mine_lo, at["far"])
    onward("b", 0, 1, mine_hi)
    onward("a", 0, 1, mine_lo)
    for name in ("right", "left"):
        for h in (0, 1) if name == "right" else (1, 0):
            mx[name, h] = net.number()
            spot = mixed_v.at[x, (lo, hi)[h]]
            net.send(mx[name, h], spot, spot, at[name])
    side(0, 0, mine_hi)
    for i, (name, back) in enumerate(
        (("right", "left"), ("left", "right"), ("over", "over")), start=1
    ):
        spot = kv.at[slot(y, z, a_x[i]), lo]
        net.got(ax[name], spot, at[back])
        net.send(a_far[i], spot, spot, at["far"])
        onward("a", i, 1, spot)
    spot = kv.at[slot(1 - y, z, x), hi]
    net.got(b_far, spot, at["far"])
    onward("b", 1, 1, spot)
    side(1, 0, spot)
    for i in range(NX):
        spot = kv.at[slot(1 - y, z, a_x[i]), lo]
        net.got(a_far[i], spot, at["far"])
        onward("a", NX + i, 1, spot)
    ring_step(4)
    wo_far = net.number()
    wo_mine, wo_other = pl.ds(y * NZ, NZ), pl.ds((1 - y) * NZ, NZ)
    net.send(wo_far, wo_v.at[wo_mine], wo_v.at[wo_mine], at["far"])

    loads[1].wait()
    acc[...] = jnp.zeros_like(acc)
    den[...] = jnp.zeros_like(den)

    def ask(b):
        q = lax.dot_general(
            mixed_v[b], wq_v[...].reshape(heads * hdim, width), (((1,), (1,)), ((), ())),
            preferred_element_type=f32,
        ).astype(bf)
        for h in range(heads):
            a = jnp.dot(q[:, h * hdim:(h + 1) * hdim], uk_v[h], preferred_element_type=f32)
            r = lax.rsqrt(jnp.mean(a * a, axis=-1, keepdims=True) + EPS)
            scaled[b, pl.ds(h * rows, rows), :] = (
                a * r * temps[x * heads + h] / lat
            ).astype(bf)

    gap = lax.broadcasted_iota(jnp.int32, (rows, rows), 1) - lax.broadcasted_iota(
        jnp.int32, (rows, rows), 0
    )

    def task(b, zz):
        bases = [slot(yy, zz, 0) for yy in range(NY)]
        k = jnp.concatenate(
            [kv[pl.ds(base, NX)].reshape(NX * rows, lat) for base in bases], axis=0
        )
        here = bo[slot(y, z, b)]
        seen = [gap <= (here - bo[base + j]) * rows for base in bases for j in range(NX)]
        n_h = 2
        for h0 in range(0, heads, n_h):
            part = pl.ds(h0 * rows, n_h * rows)
            s = lax.dot_general(
                scaled[b, part, :], k, (((1,), (1,)), ((), ())), preferred_element_type=f32
            )
            p = jnp.exp(s)
            p = jnp.concatenate(
                [
                    jnp.concatenate(
                        [
                            jnp.where(
                                seen[j],
                                p[h * rows:(h + 1) * rows, j * rows:(j + 1) * rows],
                                0.0,
                            )
                            for j in range(len(seen))
                        ],
                        axis=1,
                    )
                    for h in range(n_h)
                ],
                axis=0,
            )
            d = p[:, 0:rows]
            for j in range(1, len(seen)):
                d = d + p[:, j * rows:(j + 1) * rows]
            den[b, part, :] += d
            acc[b, part, :] += jnp.dot(p.astype(bf), k, preferred_element_type=f32)

    turns = [(c, w) for c in range(2) for w in (1, 2)]

    def signed(k, w):
        return k if w == 1 else -k

    ask(x)
    spot = mixed_v.at[xs(3), lo]
    net.got(mx["right", 0], spot, at["left"])
    m_up = net.number()
    net.send(m_up, spot, spot, at["right"])
    spot = mixed_v.at[xs(1), hi]
    net.got(mx["left", 1], spot, at["right"])
    m_down = net.number()
    net.send(m_down, spot, spot, at["left"])
    relay(0, 0)
    relay(1, 0)
    piece(1, 0, 1)
    piece(1, 0, 2)
    ended(0, 0)
    ended(1, 0)
    task(x, z)
    piece(1, 1, 1)
    piece(1, 1, 2)
    net.got(mx["right", 1], mixed_v.at[xs(3), hi], at["left"])
    ask(xs(3))
    relay(0, 1)
    relay(0, -1)
    task(xs(3), z)
    net.got(mx["left", 0], mixed_v.at[xs(1), lo], at["right"])
    ask(xs(1))
    relay(1, 1)
    relay(1, -1)
    task(xs(1), z)
    net.got(m_up, mixed_v.at[xs(2), lo], at["left"])
    net.got(m_down, mixed_v.at[xs(2), hi], at["right"])
    ask(xs(2))
    task(xs(2), z)

    rounds = (
        (1, 1, [functools.partial(piece, 2, c, w) for c, w in turns]),
        (1, 2, [functools.partial(relay, c, signed(2, w)) for c, w in turns]),
        (2, 1, [functools.partial(piece, 3, c, w) for c, w in turns]),
        (2, 2, [functools.partial(relay, c, signed(3, w)) for c, w in turns]),
    )
    for k, w, between in rounds:
        for c in range(2):
            ended(c, signed(k, w))
        zz = tile_of(0, signed(k, w))[2]

        def one(b, _, between=between, zz=zz):
            for j, act in enumerate(between):
                pl.when(b == j)(act)
            task(b, zz)
            return 0

        lax.fori_loop(0, NX, one, 0)

    last = [(0, 4), (1, -4)]

    def arrive_three():
        for c, w in turns:
            ended(c, signed(3, w))

    def arrive_four():
        for c, w in turns:
            piece(4, c, w)
        for c, tag in last:
            relay(c, tag)

    def arrive_last():
        for c, tag in last:
            ended(c, tag)

    def last_tiles(b, before=()):
        def one(i, _):
            for j, act in enumerate(before):
                pl.when(i == j)(act)
            task(b, lax.rem(z + 3 + 2 * i - 3 * (i // 2), NZ))
            return 0

        lax.fori_loop(0, 3, one, 0)
        for h in range(heads):
            part = pl.ds(h * rows, rows)
            d = jnp.sum(den[b, part, :], axis=-1, keepdims=True)
            ctx = (acc[b, part, :] / d).astype(bf)
            ho[:, h * hdim:(h + 1) * hdim] = jnp.dot(
                ctx, uv_v[h], preferred_element_type=f32
            ).astype(bf)

    def project():
        return jnp.dot(
            ho[...], wo_v[...].reshape(heads * hdim, width), preferred_element_type=f32
        )

    loads[2].wait()
    last_tiles(xs(2), (arrive_three, arrive_four, arrive_last))
    net.got(wo_far, wo_v.at[wo_other], at["far"])
    po[0] = project().astype(bf)
    out_n = [net.number() for _ in range(4)]
    net.send(out_n[0], po.at[0, lo], passing.at[0], at["right"])
    net.send(out_n[1], po.at[0, hi], passing.at[1], at["left"])
    last_tiles(xs(1))
    net.got(out_n[0], passing.at[0], at["left"])
    res = project()
    po[1, lo] = (res[:half] + passing[0].astype(f32)).astype(bf)
    po[1, hi] = res[half:].astype(bf)
    net.send(out_n[2], po.at[1], landed.at[0], at["right"])
    last_tiles(xs(3))
    net.got(out_n[1], passing.at[1], at["right"])
    res = project()
    po[2, lo] = res[:half].astype(bf)
    po[2, hi] = (res[half:] + passing[1].astype(f32)).astype(bf)
    net.send(out_n[3], po.at[2], landed.at[1], at["left"])
    last_tiles(x)
    res = project()
    net.got(out_n[2], landed.at[0], at["left"])
    net.got(out_n[3], landed.at[1], at["right"])
    out[...] = (res + landed[0].astype(f32) + landed[1].astype(f32)).astype(out.dtype)
    for a, ok, c, n in shifts:
        pl.when(ok)(c.wait_send)
    for dst, n, c, own in moves:
        pl.when(away)(c.wait_send)
    net.drain(at["far"])
    assert net.count == N_COPIES, net.count


N_COPIES = 2 + 3 + 1 + 14 + 7 + 3 + 4 + 56 + 1 + 14 + 48 + 6 + 1 + 4


def tick(bo, temps, depth_temp, embedded, probe, wq, wo, recent, w_latent, w_uk, w_uv):
    rows, width = embedded.shape
    n_heads, hdim, lat = w_uk.shape
    heads = n_heads // NX
    any_ = pl.BlockSpec(memory_space=pl.ANY)
    smem = pl.BlockSpec(memory_space=pltpu.SMEM)
    vmem = pl.BlockSpec(memory_space=pltpu.VMEM)
    bf, f32 = jnp.bfloat16, jnp.float32
    return pl.pallas_call(
        tick_kernel,
        out_shape=jax.ShapeDtypeStruct((rows, width), bf),
        in_specs=[smem] * 3 + [vmem] * 4 + [any_] * 4,
        out_specs=vmem,
        scratch_shapes=[
            pltpu.VMEM(recent.shape, bf),
            pltpu.VMEM((rows, width), f32),
            pltpu.VMEM((rows, 128), f32),
            pltpu.VMEM(w_latent.shape, bf),
            pltpu.VMEM((GROUP,) + wq.shape, bf),
            pltpu.VMEM((GROUP,) + wo.shape, bf),
            pltpu.VMEM((heads, hdim, lat), bf),
            pltpu.VMEM((heads, lat, hdim), bf),
            pltpu.VMEM((NX, rows, width), bf),
            pltpu.VMEM((bo.shape[0], rows, lat), bf),
            pltpu.VMEM((NX, heads * rows, lat), bf),
            pltpu.VMEM((NX, heads * rows, lat), f32),
            pltpu.VMEM((NX, heads * rows, rows), f32),
            pltpu.VMEM((rows, heads * hdim), bf),
            pltpu.VMEM((3, rows, width), bf),
            pltpu.VMEM((2, rows // 2, width), bf),
            pltpu.VMEM((2, rows, width), bf),
            pltpu.SemaphoreType.DMA((N_COPIES,)),
            pltpu.SemaphoreType.DMA((N_COPIES,)),
            pltpu.SemaphoreType.DMA((3,)),
        ],
        compiler_params=pltpu.CompilerParams(
            collective_id=0, has_side_effects=True, vmem_limit_bytes=60 << 20
        ),
        name="tick",
    )(bo, temps, depth_temp, embedded, probe, wq, wo, recent, w_latent, w_uk, w_uv)


def shards(
    embedded, recent, query_depth, depth_temp, w_latent, w_query, w_uk, attn_temp, w_uv,
    w_out, block_offsets,
):
    return tick(
        block_offsets, attn_temp[0], depth_temp, embedded[0], query_depth,
        jnp.swapaxes(w_query[0], 0, 1), w_out[0], recent[0], w_latent[0], w_uk[0], w_uv[0],
    )[None]


def solution(mesh):
    in_specs = (
        P("sec", "seq", None),
        P("sec", None, "seq", None),
        P("sec", None),
        P("sec"),
        P("sec", None, None),
        P("sec", None, "seq"),
        P("sec", None, None, None),
        P("sec", None),
        P("sec", None, None, None),
        P("sec", "seq", None),
        P(),
    )
    return jax.shard_map(
        shards, mesh=mesh, in_specs=in_specs, out_specs=P("sec", "seq", None), check_vma=False
    )
```

```python
import functools

import jax
import jax.numpy as jnp
from jax import lax
from jax.experimental import pallas as pl
from jax.experimental.pallas import tpu as pltpu
from jax.sharding import PartitionSpec as P

MESH = pl.DeviceIdType.MESH
EPS = 1e-06
NY, NZ, NX = 2, 8, 4
GROUP = NY * NZ


def place():
    sec = lax.axis_index("sec")
    seq = lax.axis_index("seq")
    return sec, seq // (NZ * NX), (seq // NX) % NZ, seq % NX


def seq_of(y, z, x):
    return (y * NZ + z) * NX + x


class Net:
    def __init__(self, ssem, rsem):
        self.ssem, self.rsem, self.count, self.sent = ssem, rsem, 0, []

    def number(self):
        self.count += 1
        return self.count - 1

    def copy(self, n, src, dst, dev):
        return pltpu.make_async_remote_copy(
            src_ref=src,
            dst_ref=dst,
            send_sem=self.ssem.at[n],
            recv_sem=self.rsem.at[n],
            device_id=dev,
            device_id_type=MESH,
        )

    def send(self, n, src, dst, dev, like=None):
        self.copy(n, src, dst, dev).start()
        self.sent.append((n, src if like is None else like))

    def got(self, n, dst, dev):
        self.copy(n, dst, dst, dev).wait_recv()

    def drain(self, dev):
        for n, like in self.sent:
            self.copy(n, like, like, dev).wait_send()


def peers():
    sec, y, z, x = place()
    return dict(
        right=(sec, seq_of(y, z, (x + 1) % NX)),
        left=(sec, seq_of(y, z, (x + 3) % NX)),
        over=(sec, seq_of(y, z, (x + 2) % NX)),
        up=(sec, seq_of(y, (z + 1) % NZ, x)),
        down=(sec, seq_of(y, (z + 7) % NZ, x)),
        far=(sec, seq_of(1 - y, z, x)),
    )


def tick_kernel(
    bo, temps, depth_temp, embedded, probe, wq, wo, recent, w_latent, w_uk, w_uv, out,
    relayed, blend, weight, lat_v, wq_v, wo_v, uk_v, uv_v, mixed_v, kv,
    scaled, acc, den, ho, po, passing, landed, ssem, rsem, lsem,
):
    sec, y, z, x = place()
    seq = slot_me = seq_of(y, z, x)
    n_sec = lax.axis_size("sec")
    at = peers()
    rows, width = embedded.shape
    _, hdim, lat = w_uk.shape
    heads = w_uk.shape[0] // NX
    half = rows // 2
    lo, hi = pl.ds(0, half), pl.ds(half, half)
    f32, bf = jnp.float32, jnp.bfloat16

    def slot(yy, zz, xx):
        return (yy * NZ + zz) * NX + xx

    def xs(i):
        return lax.rem(x + i, NX)

    mine_heads = pl.ds(x * heads, heads)
    loads = [
        pltpu.make_async_copy(a, b, lsem.at[i])
        for i, (a, b) in enumerate(
            ((w_latent, lat_v), (w_uk.at[mine_heads], uk_v), (w_uv.at[mine_heads], uv_v))
        )
    ]
    for c in loads:
        c.start()

    group, rank = seq // GROUP, seq % GROUP
    owner = rank * NX + group
    source = x * GROUP + seq // NX
    mine = seq // NX
    away = owner != seq
    owner_2 = seq_of(1 - rank // NZ, rank % NZ, group)
    mine_2 = (1 - y) * NZ + z
    source_2 = x * GROUP + mine_2
    away_2 = owner_2 != seq
    barrier = pltpu.get_barrier_semaphore()
    names = ("right", "left", "over", "up", "down", "far")
    for name in names:
        pl.semaphore_signal(barrier, inc=1, device_id=at[name], device_id_type=MESH)
    for a in range(1, n_sec):
        pl.semaphore_signal(
            barrier, inc=1, device_id=(lax.rem(sec + a, n_sec), seq), device_id_type=MESH
        )

    @pl.when(away)
    def _():
        pl.semaphore_signal(barrier, inc=1, device_id=(sec, source), device_id_type=MESH)

    @pl.when(away_2)
    def _():
        pl.semaphore_signal(barrier, inc=1, device_id=(sec, source_2), device_id_type=MESH)

    pl.semaphore_wait(
        barrier,
        len(names) + n_sec - 1 + away.astype(jnp.int32) + away_2.astype(jnp.int32),
    )

    net = Net(ssem, rsem)

    moves = []

    def hand_over(src, dst, to, here, off):
        n = net.number()
        c = net.copy(n, src, dst.at[rank], (sec, to))
        own = pltpu.make_async_copy(src, dst.at[here], ssem.at[n])
        pl.when(off)(c.start)
        pl.when(jnp.logical_not(off))(own.start)
        moves.append((off, c))

        def taken(origin):
            spot = dst.at[here]

            @pl.when(off)
            def _():
                net.copy(n, spot, spot, (sec, origin)).wait_recv()

            pl.when(jnp.logical_not(off))(own.wait)
            return spot

        return taken

    near_q = hand_over(wq, wq_v, owner, mine, away)
    other_q = hand_over(wq, wq_v, owner_2, mine_2, away_2)
    ring_up, ring_down, crossed, ready = {}, {}, {}, []

    def cross(tag, spot):
        crossed[tag] = net.number()
        net.send(crossed[tag], spot, spot, at["far"])

    def ring(i, d, k, spot, ways=3):
        last_up = 4 if d == 0 else 3
        if ways & 1 and k <= last_up:
            ring_up[i, d, k] = net.number()
            net.send(ring_up[i, d, k], spot, spot, at["up"])
        if ways & 2 and k <= 7 - last_up:
            ring_down[i, d, k] = net.number()
            net.send(ring_down[i, d, k], spot, spot, at["down"])

    def ring_step(k, i, dst):
        for d in range(2):
            yy = y if d == 0 else 1 - y
            if (i, d, k) in ring_up:
                spot = dst.at[yy * NZ + lax.rem(z + NZ - k, NZ)]
                net.got(ring_up[i, d, k], spot, at["down"])
                ring(i, d, k + 1, spot, 1)
                if i == 1:
                    ready.append((k, spot))
            if (i, d, k) in ring_down:
                spot = dst.at[yy * NZ + lax.rem(z + k, NZ)]
                net.got(ring_down[i, d, k], spot, at["up"])
                ring(i, d, k + 1, spot, 2)
                if i == 1:
                    ready.append((-k, spot))

    def ring_q(k):
        ring_step(k, 0, wq_v)

    def ring_o(k):
        ring_step(k, 1, wo_v)

    ring(0, 0, 1, near_q(source))
    ring(0, 1, 1, other_q(source_2))
    near_o = hand_over(wo, wo_v, owner, mine, away)
    shifts = []
    for a in range(1, n_sec):
        n = net.number()
        ok = sec + a < n_sec
        c = net.copy(
            n, recent.at[a - 1], relayed.at[a - 1], (lax.rem(sec + a, n_sec), seq)
        )
        pl.when(ok)(c.start)
        shifts.append((a, ok, c, n))
    asked = probe[...]
    scale = (
        depth_temp[0] * lax.rsqrt(jnp.mean(asked * asked, axis=-1, keepdims=True) + EPS) / width
    )
    step_rows = 16

    def add_source(read, fresh):
        def some(i, _):
            part = pl.ds(pl.multiple_of(i * step_rows, step_rows), step_rows)
            v = read(part).astype(f32)
            norm = lax.rsqrt(jnp.mean(v * v, axis=-1, keepdims=True) + EPS)
            w = jnp.exp(scale * jnp.sum(v * asked, axis=-1, keepdims=True) * norm)
            if fresh:
                blend[part, :] = w * v
                weight[part, :] = jnp.broadcast_to(w, (step_rows, 128))
            else:
                blend[part, :] += w * v
                weight[part, :] += jnp.broadcast_to(w, (step_rows, 128))
            return 0

        lax.fori_loop(0, rows // step_rows, some, 0)

    add_source(lambda part: embedded[part, :], True)
    ring_q(1)
    spot_o = near_o(source)
    ring(1, 0, 1, spot_o)
    ready.append((0, spot_o))
    ring_q(2)
    ring_o(1)
    ring_q(3)
    for a, ok, c, n in shifts:

        @pl.when(sec >= a)
        def _():
            net.copy(
                n,
                relayed.at[a - 1],
                relayed.at[a - 1],
                (lax.rem(sec + n_sec - a, n_sec), seq),
            ).wait_recv()
            add_source(lambda part: relayed[a - 1, part, :], False)

    def finish(i, _):
        part = pl.ds(pl.multiple_of(i * step_rows, step_rows), step_rows)
        mixed_v[x, part, :] = (blend[part, :] / weight[part, 0:1]).astype(bf)
        return 0

    lax.fori_loop(0, rows // step_rows, finish, 0)
    loads[0].wait()
    latent = jnp.dot(mixed_v[x], lat_v[...], preferred_element_type=f32)
    kv[slot_me] = (
        latent * lax.rsqrt(jnp.mean(latent * latent, axis=-1, keepdims=True) + EPS)
    ).astype(bf)

    up_n, down_n, bx, bxx, ax, mx = {}, {}, {}, {}, {}, {}
    some_half = kv.at[0, lo]

    def onward(kind, c, k, spot, ways=3):
        last_up = 4 if c % 2 == 0 else 3
        if ways & 1 and k <= last_up:
            up_n[kind, c, k] = net.number()
            net.send(up_n[kind, c, k], spot, spot, at["up"], some_half)
        if ways & 2 and k <= 7 - last_up:
            down_n[kind, c, k] = net.number()
            net.send(down_n[kind, c, k], spot, spot, at["down"], some_half)

    def side(c, k, spot):
        for name in ("right", "left"):
            bx[c, k, name] = net.number()
            net.send(bx[c, k, name], spot, spot, at[name], some_half)

    def tile_of(c, tag):
        yy = y if c == 0 else 1 - y
        return c, yy, lax.rem(z + NZ - tag, NZ), tag

    def relay(c, tag):
        _, yy, zz, _ = tile_of(c, tag)
        r = kv.at[slot(yy, zz, xs(3)), hi]
        l = kv.at[slot(yy, zz, xs(1)), hi]
        net.got(bx[c, tag, "right"], r, at["left"])
        net.got(bx[c, tag, "left"], l, at["right"])
        bxx[c, tag] = net.number()
        if (c + tag) % 2 == 0:
            net.send(bxx[c, tag], r, r, at["right"], some_half)
        else:
            net.send(bxx[c, tag], l, l, at["left"], some_half)

    def ended(c, tag):
        _, yy, zz, _ = tile_of(c, tag)
        spot = kv.at[slot(yy, zz, xs(2)), hi]
        net.got(bxx[c, tag], spot, at["left"] if (c + tag) % 2 == 0 else at["right"])

    a_x = {0: x, 1: xs(3), 2: xs(1), 3: xs(2)}

    def piece(k, c, way):
        table, back = (up_n, "down") if way == 1 else (down_n, "up")
        tag = k if way == 1 else -k
        _, yy, zz, _ = tile_of(c, tag)
        if ("b", c, k) in table:
            spot = kv.at[slot(yy, zz, x), hi]
            net.got(table["b", c, k], spot, at[back])
            onward("b", c, k + 1, spot, way)
            side(c, tag, spot)
        for i in range(NX):
            n = ("a", c * NX + i, k)
            if n in table:
                spot = kv.at[slot(yy, zz, a_x[i]), lo]
                net.got(table[n], spot, at[back])
                onward("a", c * NX + i, k + 1, spot, way)

    ring_q(4)
    ring_o(2)
    mine_lo, mine_hi = kv.at[slot_me, lo], kv.at[slot_me, hi]
    for name in ("right", "left", "over"):
        ax[name] = net.number()
        net.send(ax[name], mine_lo, mine_lo, at[name])
    b_far = net.number()
    net.send(b_far, mine_hi, mine_hi, at["far"])
    a_far = [net.number() for _ in range(NX)]
    net.send(a_far[0], mine_lo, mine_lo, at["far"])
    onward("b", 0, 1, mine_hi)
    onward("a", 0, 1, mine_lo)
    for name in ("right", "left"):
        for h in (0, 1) if name == "right" else (1, 0):
            mx[name, h] = net.number()
            spot = mixed_v.at[x, (lo, hi)[h]]
            net.send(mx[name, h], spot, spot, at[name])
    side(0, 0, mine_hi)
    for i, (name, back) in enumerate(
        (("right", "left"), ("left", "right"), ("over", "over")), start=1
    ):
        spot = kv.at[slot(y, z, a_x[i]), lo]
        net.got(ax[name], spot, at[back])
        net.send(a_far[i], spot, spot, at["far"])
        onward("a", i, 1, spot)
    spot = kv.at[slot(1 - y, z, x), hi]
    net.got(b_far, spot, at["far"])
    onward("b", 1, 1, spot)
    side(1, 0, spot)
    for i in range(NX):
        spot = kv.at[slot(1 - y, z, a_x[i]), lo]
        net.got(a_far[i], spot, at["far"])
        onward("a", NX + i, 1, spot)

    ring_o(3)
    ring_o(4)
    for tag, spot in ready:
        cross(tag, spot)
    loads[1].wait()
    acc[...] = jnp.zeros_like(acc)
    den[...] = jnp.zeros_like(den)

    def ask(b):
        q = lax.dot_general(
            mixed_v[b], wq_v[...].reshape(heads * hdim, width), (((1,), (1,)), ((), ())),
            preferred_element_type=f32,
        ).astype(bf)
        for h in range(heads):
            a = jnp.dot(q[:, h * hdim:(h + 1) * hdim], uk_v[h], preferred_element_type=f32)
            r = lax.rsqrt(jnp.mean(a * a, axis=-1, keepdims=True) + EPS)
            scaled[b, pl.ds(h * rows, rows), :] = (
                a * r * temps[x * heads + h] / lat
            ).astype(bf)

    gap = lax.broadcasted_iota(jnp.int32, (rows, rows), 1) - lax.broadcasted_iota(
        jnp.int32, (rows, rows), 0
    )

    def task(b, zz):
        bases = [slot(yy, zz, 0) for yy in range(NY)]
        k = jnp.concatenate(
            [kv[pl.ds(base, NX)].reshape(NX * rows, lat) for base in bases], axis=0
        )
        here = bo[slot(y, z, b)]
        seen = [gap <= (here - bo[base + j]) * rows for base in bases for j in range(NX)]
        n_h = 2
        for h0 in range(0, heads, n_h):
            part = pl.ds(h0 * rows, n_h * rows)
            s = lax.dot_general(
                scaled[b, part, :], k, (((1,), (1,)), ((), ())), preferred_element_type=f32
            )
            p = jnp.exp(s)
            p = jnp.concatenate(
                [
                    jnp.concatenate(
                        [
                            jnp.where(
                                seen[j],
                                p[h * rows:(h + 1) * rows, j * rows:(j + 1) * rows],
                                0.0,
                            )
                            for j in range(len(seen))
                        ],
                        axis=1,
                    )
                    for h in range(n_h)
                ],
                axis=0,
            )
            d = p[:, 0:rows]
            for j in range(1, len(seen)):
                d = d + p[:, j * rows:(j + 1) * rows]
            den[b, part, :] += d
            acc[b, part, :] += jnp.dot(p.astype(bf), k, preferred_element_type=f32)

    turns = [(c, w) for c in range(2) for w in (1, 2)]

    def signed(k, w):
        return k if w == 1 else -k

    ask(x)
    spot = mixed_v.at[xs(3), lo]
    net.got(mx["right", 0], spot, at["left"])
    m_up = net.number()
    net.send(m_up, spot, spot, at["right"])
    spot = mixed_v.at[xs(1), hi]
    net.got(mx["left", 1], spot, at["right"])
    m_down = net.number()
    net.send(m_down, spot, spot, at["left"])
    relay(0, 0)
    relay(1, 0)
    piece(1, 0, 1)
    piece(1, 0, 2)
    ended(0, 0)
    ended(1, 0)
    task(x, z)
    piece(1, 1, 1)
    piece(1, 1, 2)
    net.got(mx["right", 1], mixed_v.at[xs(3), hi], at["left"])
    ask(xs(3))
    relay(0, 1)
    relay(0, -1)
    task(xs(3), z)
    net.got(mx["left", 0], mixed_v.at[xs(1), lo], at["right"])
    ask(xs(1))
    relay(1, 1)
    relay(1, -1)
    task(xs(1), z)
    net.got(m_up, mixed_v.at[xs(2), lo], at["left"])
    net.got(m_down, mixed_v.at[xs(2), hi], at["right"])
    ask(xs(2))
    task(xs(2), z)

    rounds = (
        (1, 1, [functools.partial(piece, 2, c, w) for c, w in turns]),
        (1, 2, [functools.partial(relay, c, signed(2, w)) for c, w in turns]),
        (2, 1, [functools.partial(piece, 3, c, w) for c, w in turns]),
        (2, 2, [functools.partial(relay, c, signed(3, w)) for c, w in turns]),
    )
    for k, w, between in rounds:
        for c in range(2):
            ended(c, signed(k, w))
        zz = tile_of(0, signed(k, w))[2]

        def one(b, _, between=between, zz=zz):
            for j, act in enumerate(between):
                pl.when(b == j)(act)
            task(b, zz)
            return 0

        lax.fori_loop(0, NX, one, 0)

    last = [(0, 4), (1, -4)]

    def arrive_three():
        for c, w in turns:
            ended(c, signed(3, w))

    def arrive_four():
        for c, w in turns:
            piece(4, c, w)
        for c, tag in last:
            relay(c, tag)

    def arrive_last():
        for c, tag in last:
            ended(c, tag)

    def last_tiles(b, before=()):
        def one(i, _):
            for j, act in enumerate(before):
                pl.when(i == j)(act)
            task(b, lax.rem(z + 3 + 2 * i - 3 * (i // 2), NZ))
            return 0

        lax.fori_loop(0, 3, one, 0)
        for h in range(heads):
            part = pl.ds(h * rows, rows)
            d = jnp.sum(den[b, part, :], axis=-1, keepdims=True)
            ctx = (acc[b, part, :] / d).astype(bf)
            ho[:, h * hdim:(h + 1) * hdim] = jnp.dot(
                ctx, uv_v[h], preferred_element_type=f32
            ).astype(bf)

    def project():
        return jnp.dot(
            ho[...], wo_v[...].reshape(heads * hdim, width), preferred_element_type=f32
        )

    loads[2].wait()
    last_tiles(xs(2), (arrive_three, arrive_four, arrive_last))
    for tag, n in crossed.items():
        net.got(n, wo_v.at[(1 - y) * NZ + lax.rem(z + NZ - tag, NZ)], at["far"])
    po[0] = project().astype(bf)
    out_n = [net.number() for _ in range(4)]
    net.send(out_n[0], po.at[0, lo], passing.at[0], at["right"])
    net.send(out_n[1], po.at[0, hi], passing.at[1], at["left"])
    last_tiles(xs(1))
    net.got(out_n[0], passing.at[0], at["left"])
    res = project()
    po[1, lo] = (res[:half] + passing[0].astype(f32)).astype(bf)
    po[1, hi] = res[half:].astype(bf)
    net.send(out_n[2], po.at[1], landed.at[0], at["right"])
    last_tiles(xs(3))
    net.got(out_n[1], passing.at[1], at["right"])
    res = project()
    po[2, lo] = res[:half].astype(bf)
    po[2, hi] = (res[half:] + passing[1].astype(f32)).astype(bf)
    net.send(out_n[3], po.at[2], landed.at[1], at["left"])
    last_tiles(x)
    res = project()
    net.got(out_n[2], landed.at[0], at["left"])
    net.got(out_n[3], landed.at[1], at["right"])
    out[...] = (res + landed[0].astype(f32) + landed[1].astype(f32)).astype(out.dtype)
    for a, ok, c, n in shifts:
        pl.when(ok)(c.wait_send)
    for off, c in moves:
        pl.when(off)(c.wait_send)
    net.drain(at["far"])
    assert net.count == N_COPIES, net.count


N_COPIES = 3 + 3 + 14 + 7 + 8 + 3 + 4 + 56 + 1 + 14 + 48 + 6 + 4


def tick(bo, temps, depth_temp, embedded, probe, wq, wo, recent, w_latent, w_uk, w_uv):
    rows, width = embedded.shape
    n_heads, hdim, lat = w_uk.shape
    heads = n_heads // NX
    any_ = pl.BlockSpec(memory_space=pl.ANY)
    smem = pl.BlockSpec(memory_space=pltpu.SMEM)
    vmem = pl.BlockSpec(memory_space=pltpu.VMEM)
    bf, f32 = jnp.bfloat16, jnp.float32
    return pl.pallas_call(
        tick_kernel,
        out_shape=jax.ShapeDtypeStruct((rows, width), bf),
        in_specs=[smem] * 3 + [vmem] * 4 + [any_] * 4,
        out_specs=vmem,
        scratch_shapes=[
            pltpu.VMEM(recent.shape, bf),
            pltpu.VMEM((rows, width), f32),
            pltpu.VMEM((rows, 128), f32),
            pltpu.VMEM(w_latent.shape, bf),
            pltpu.VMEM((GROUP,) + wq.shape, bf),
            pltpu.VMEM((GROUP,) + wo.shape, bf),
            pltpu.VMEM((heads, hdim, lat), bf),
            pltpu.VMEM((heads, lat, hdim), bf),
            pltpu.VMEM((NX, rows, width), bf),
            pltpu.VMEM((bo.shape[0], rows, lat), bf),
            pltpu.VMEM((NX, heads * rows, lat), bf),
            pltpu.VMEM((NX, heads * rows, lat), f32),
            pltpu.VMEM((NX, heads * rows, rows), f32),
            pltpu.VMEM((rows, heads * hdim), bf),
            pltpu.VMEM((3, rows, width), bf),
            pltpu.VMEM((2, rows // 2, width), bf),
            pltpu.VMEM((2, rows, width), bf),
            pltpu.SemaphoreType.DMA((N_COPIES,)),
            pltpu.SemaphoreType.DMA((N_COPIES,)),
            pltpu.SemaphoreType.DMA((3,)),
        ],
        compiler_params=pltpu.CompilerParams(
            collective_id=0, has_side_effects=True, vmem_limit_bytes=60 << 20
        ),
        name="tick",
    )(bo, temps, depth_temp, embedded, probe, wq, wo, recent, w_latent, w_uk, w_uv)


def shards(
    embedded, recent, query_depth, depth_temp, w_latent, w_query, w_uk, attn_temp, w_uv,
    w_out, block_offsets,
):
    return tick(
        block_offsets, attn_temp[0], depth_temp, embedded[0], query_depth,
        jnp.swapaxes(w_query[0], 0, 1), w_out[0], recent[0], w_latent[0], w_uk[0], w_uv[0],
    )[None]


def solution(mesh):
    in_specs = (
        P("sec", "seq", None),
        P("sec", None, "seq", None),
        P("sec", None),
        P("sec"),
        P("sec", None, None),
        P("sec", None, "seq"),
        P("sec", None, None, None),
        P("sec", None),
        P("sec", None, None, None),
        P("sec", "seq", None),
        P(),
    )
    return jax.shard_map(
        shards, mesh=mesh, in_specs=in_specs, out_specs=P("sec", "seq", None), check_vma=False
    )
```
